32 devices in a mesh: prow: 16 (over z, y, x), pcol: 2 (over core).
Axes of the slice: x: 2, y: 2, z: 4, core: 2. Of those that a mesh axis runs over, the one named last changes fastest.
Arguments:
- right_sides: float32 [32, 1, 4096], P(None, None, 'prow'), may hold values from -6 to 6
- factor: bfloat16 [1, 4096, 8, 512], P(None, 'prow', None, 'pcol'), as said below
- node_sizes: int32 [7], replicated, may hold values from 1 to 9, 16 in all
- row_blocks: int32 [7, 16], replicated, may hold values 0 or 1
Outputs:
- forward: float32 [32, 1, 4096], P(None, None, 'prow')
- solution: float32 [32, 8, 512], P(None, None, 'pcol')
The draws below stay inside these ranges and needn't reach their ends.
Inputs may be any that keep to these rules, and one draw needn't show every extreme that they name: factor is zero above its diagonal; its diagonal lies between 0.5 and 1. `row_blocks`: flags of tiles that belong to no proper ancestor of the supernode are ignored.
All inputs are finite; a program needn't handle non-finite values.
Results may differ from the reference program's by a relative error of at most 0.0047.
Values may be sent and summed in bfloat16 or wider, within the bound.
A program may use at most 64 MiB of HBM per device.

```python
import math
import jax
import jax.numpy as jnp
import numpy as np
from jax import lax

B = 256
RHS = 32
LEVELS = 3
RT = 1
SN = 7
NT = 16
CT = 8
WMAX = 9
N_PROW = 16
N_PCOL = 2


def draw_factor(key, part):
    order_len = NT * B
    key_off, key_diag = jax.random.split(key, 2)

    def one_block(block_id):
        block_key = jax.random.fold_in(key_off, block_id)
        diag_key = jax.random.fold_in(key_diag, block_id)
        spread = jax.random.truncated_normal(block_key, -4.0, 4.0, (B, order_len), jnp.float32)
        spread = spread * (1.5 / order_len ** 0.5)
        diag_vals = jax.random.uniform(diag_key, (B,), jnp.float32, 0.5, 1.0)
        row_ids = block_id * B + jnp.arange(B, dtype=jnp.int32)
        col_ids = jnp.arange(order_len, dtype=jnp.int32)
        values = jnp.where(col_ids[None, :] > row_ids[:, None], 0.0, spread)
        values = jnp.where(col_ids[None, :] == row_ids[:, None], diag_vals[:, None], values)
        return values
    blocks = lax.map(one_block, jnp.arange(NT, dtype=jnp.int32))
    return blocks.reshape(RT, order_len // RT, CT, order_len // CT).astype(jnp.bfloat16)


def touch_ends(array, rng, least, largest):
    longest = array.shape.index(max(array.shape))
    spots = []
    for shift in (0, 1):
        where = [jax.random.randint(jax.random.fold_in(rng, axis), (), 0, length) for axis, length in enumerate(array.shape)]
        where[longest] = (where[longest] + shift) % array.shape[longest]
        spots.append(tuple(where))
    return array.at[spots[0]].set(least).at[spots[1]].set(largest)


def levels(stream_key, extent, cuts, low, top_value):
    def one(position, shards_of):
        draws = jax.random.uniform(jax.random.fold_in(jax.random.fold_in(stream_key, 6), position), (shards_of,), jnp.float32, low / len(cuts), top_value / len(cuts))
        return jnp.repeat(jnp.exp(draws), extent[position] // shards_of).reshape((-1,) + (1,) * (len(extent) - position - 1))

    gain = one(*cuts[0])
    for cut in cuts[1:]:
        gain = gain * one(*cut)
    return gain


def profile(amount, total, bound, lean):
    weights = [(1 << 20) // math.isqrt(rank ** lean) + 1 for rank in range(2, amount + 1)]
    spare, holding = total - bound - (amount - 1), [1] * (amount - 1)
    while spare > 0:
        free = [i for i in range(amount - 1) if holding[i] < bound]
        mass, left = sum([weights[i] for i in free]), spare
        for i in free:
            more = min(bound - holding[i], max(1, left * weights[i] // mass), spare)
            holding[i] = holding[i] + more
            spare = spare - more
    return np.array([bound] + holding)


def uneven(own_key, amount, total, reach, skew):
    if amount == 2:
        one = jax.random.randint(own_key, (), max(1, total - reach), min(reach, total - 1) + 1)
        return jnp.stack([one, total - one])
    sizes = jnp.asarray(profile(amount, total, reach, skew), jnp.int32)
    couples = (amount - 1) // 2
    donor, taker = sizes[1:1 + 2 * couples:2], sizes[2:2 + 2 * couples:2]
    margin = jnp.minimum(donor - 1, reach - taker)
    passed = jax.random.randint(jax.random.fold_in(own_key, 1), (couples,), 0, 1 << 20) % (margin + 1)
    sizes = sizes.at[1:1 + 2 * couples:2].set(donor - passed).at[2:2 + 2 * couples:2].set(taker + passed)
    return sizes[jax.random.permutation(jax.random.fold_in(own_key, 2), amount)]


def centred(rng, shape, scale, limit, pieces=(), held_as=jnp.bfloat16):
    drawn = jax.random.normal(rng, shape, jnp.float32) * scale
    if len(pieces) > 0:
        drawn = levels(rng, shape, pieces, -0.22, 0.18) * drawn
    return jnp.clip(drawn, min=-limit, max=limit).astype(held_as)


def setup_inputs(seed: int = 0) -> dict:
    seeds = jax.random.split(jax.random.key(seed), 5)
    return {
        "right_sides": centred(seeds[0], (RHS, RT, N_PROW * B), 1.0, 6.0, ((2, 16),), jnp.float32),
        "factor": draw_factor(jax.random.fold_in(seeds[4], 71), 0),
        "node_sizes": uneven(seeds[2], SN, NT, WMAX, 1).astype(jnp.int32),
        "row_blocks": touch_ends((jax.random.randint(seeds[3], (SN, NT), 0, 2) < 1).astype(jnp.int32), jax.random.fold_in(seeds[3], 1), 0, 1),
    }


def tree_tables(node_sizes, row_blocks):
    node_count = node_sizes.shape[0]
    tile_count = row_blocks.shape[1]
    tile_ends = jnp.cumsum(node_sizes).astype(jnp.int32)
    tile_starts = (tile_ends - node_sizes).astype(jnp.int32)
    tile_ids = jnp.arange(tile_count, dtype=jnp.int32)
    node_of = jnp.sum((tile_ends[None, :] <= tile_ids[:, None]).astype(jnp.int32), axis=1).astype(jnp.int32)
    heap_label = (node_count - jnp.arange(node_count, dtype=jnp.int32)).astype(jnp.int32)
    node_depth = jnp.zeros((node_count,), jnp.int32)
    for exponent in range(1, LEVELS):
        node_depth = node_depth + (heap_label >= 2 ** exponent).astype(jnp.int32)
    gap_depth = jnp.maximum(node_depth[None, :] - node_depth[:, None], 0).astype(jnp.int32)
    ancestor = (node_depth[:, None] < node_depth[None, :]) & (jnp.right_shift(heap_label[None, :], gap_depth) == heap_label[:, None])
    return tile_starts, node_of, ancestor


def reference(right_sides, factor, node_sizes, row_blocks):
    full_order = NT * B
    window_len = WMAX * B
    matrix = factor.reshape(full_order, full_order)
    tile_starts, node_of, ancestor = tree_tables(node_sizes, row_blocks)
    linked = ancestor[node_of][:, node_of] & (row_blocks[node_of, :].T == 1)

    def window_of(tile_id):
        window_start = jnp.minimum(tile_starts[node_of[tile_id]] * B, full_order - window_len).astype(jnp.int32)
        positions = window_start + jnp.arange(window_len, dtype=jnp.int32)
        inside = node_of[positions // B] == node_of[tile_id]
        return window_start, inside

    def forward_step(counter, loop_state):
        residual, solved = loop_state
        tile_id = jnp.asarray(counter).astype(jnp.int32)
        window_start, inside = window_of(tile_id)
        diag_rows = lax.dynamic_slice(matrix, (tile_id * B, window_start), (B, window_len))
        segment = lax.dynamic_slice(residual, (jnp.int32(0), window_start), (RHS, window_len))
        segment = jnp.where(inside[None, :], segment, 0.0).astype(jnp.bfloat16)
        answer = jnp.dot(segment, diag_rows.T, preferred_element_type=jnp.float32)
        solved = lax.dynamic_update_slice(solved, answer, (jnp.int32(0), tile_id * B))
        column = lax.dynamic_slice(matrix, (jnp.int32(0), tile_id * B), (full_order, B))
        rows_on = jnp.repeat(linked[:, tile_id], B)
        product = jnp.dot(answer.astype(jnp.bfloat16), column.T, preferred_element_type=jnp.float32)
        residual = residual - jnp.where(rows_on[None, :], product, 0.0)
        return residual, solved

    start_state = (right_sides.reshape(RHS, full_order).astype(jnp.float32), jnp.zeros((RHS, full_order), jnp.float32))
    residual, forward = lax.fori_loop(0, NT, forward_step, start_state)

    def backward_step(counter, loop_state):
        residual, solved = loop_state
        tile_id = (NT - 1 - jnp.asarray(counter)).astype(jnp.int32)
        window_start, inside = window_of(tile_id)
        diag_cols = lax.dynamic_slice(matrix, (window_start, tile_id * B), (window_len, B))
        segment = lax.dynamic_slice(residual, (jnp.int32(0), window_start), (RHS, window_len))
        segment = jnp.where(inside[None, :], segment, 0.0).astype(jnp.bfloat16)
        answer = jnp.dot(segment, diag_cols, preferred_element_type=jnp.float32)
        solved = lax.dynamic_update_slice(solved, answer, (jnp.int32(0), tile_id * B))
        row_slab = lax.dynamic_slice(matrix, (tile_id * B, jnp.int32(0)), (B, full_order))
        cols_on = jnp.repeat(linked[tile_id, :], B)
        product = jnp.dot(answer.astype(jnp.bfloat16), row_slab, preferred_element_type=jnp.float32)
        residual = residual - jnp.where(cols_on[None, :], product, 0.0)
        return residual, solved

    rounded = lax.optimization_barrier(forward.astype(jnp.bfloat16))
    back_state = (rounded.astype(jnp.float32), jnp.zeros((RHS, full_order), jnp.float32))
    residual, solution = lax.fori_loop(0, NT, backward_step, back_state)
    return forward.reshape(RHS, RT, N_PROW * B), solution.reshape(RHS, CT, N_PCOL * B)
```

```python
import functools

import jax
import jax.numpy as jnp
from jax import lax
from jax.experimental import pallas as pl
from jax.experimental.pallas import tpu as pltpu
from jax.sharding import PartitionSpec as P

MESH = pl.DeviceIdType.MESH
NT_DIMS = (((1,), (1,)), ((), ()))
NN_DIMS = (((1,), (0,)), ((), ()))


def kernel(
    R, C, CT, LEVELS,
    sizes_ref, blocks_ref, b_ref, a_ref,
    fwd_ref, sol_ref,
    ag_src, ag_buf, comb_buf, rs_src, rs_buf, share_buf, fin_src, fin_buf,
    ag_send, ag_recv, comb_send, comb_recv, rs_send, rs_recv,
    share_send, share_recv, fin_send, fin_recv,
):
    SN = sizes_ref.shape[0]
    me = lax.axis_index("prow")
    col = lax.axis_index("pcol")
    mine = lax.rem(me, C) == col
    slot = me // C
    before = (me + C - 1 - col) // C
    T = b_ref.shape[2]

    ag_buf[...] = jnp.zeros_like(ag_buf)
    rs_buf[...] = jnp.zeros_like(rs_buf)

    barrier = pltpu.get_barrier_semaphore()

    def greet_row(step, carry):
        pl.semaphore_signal(
            barrier, inc=1, device_id=(lax.rem(me + step, R), col), device_id_type=MESH
        )
        return carry

    def greet_col(step, carry):
        pl.semaphore_signal(
            barrier, inc=1, device_id=(me, lax.rem(col + step, C)), device_id_type=MESH
        )
        return carry

    lax.fori_loop(1, R, greet_row, 0)
    lax.fori_loop(1, C, greet_col, 0)

    ends = []
    total = jnp.int32(0)
    for s in range(SN):
        total = total + sizes_ref[s]
        ends.append(total)

    def node_of(tile):
        count = jnp.int32(0)
        for s in range(SN):
            count = count + jnp.where(ends[s] <= tile, 1, 0)
        return jnp.minimum(count, SN - 1)

    row_node = node_of(me)
    row_label = SN - row_node
    row_level = jnp.int32(0)
    for e in range(1, LEVELS):
        row_level = row_level + jnp.where(row_label >= 2**e, 1, 0)
    same, linked = [], []
    for s in range(CT):
        node = node_of(s * C + col)
        label = SN - node
        above = jnp.int32(0)
        for gap in range(1, LEVELS):
            above = above + jnp.where(jnp.right_shift(label, gap) == row_label, 1, 0)
        flag = jnp.where(blocks_ref[node, me] == 1, 1, 0)
        same.append(node == row_node)
        linked.append(above * flag > 0)

    b = b_ref[:, 0, :]
    pl.semaphore_wait(barrier, R - 1 + C - 1)

    def ag_copy(rnd, k):
        return pltpu.make_async_remote_copy(
            src_ref=ag_src.at[rnd], dst_ref=ag_buf.at[rnd, slot],
            send_sem=ag_send.at[k], recv_sem=ag_recv.at[rnd, slot],
            device_id=(k, col), device_id_type=MESH,
        )

    def gather(rnd, value):
        @pl.when(mine)
        def _():
            if rnd > 0:
                lax.fori_loop(
                    me + 1, R, lambda k, x: (ag_copy(rnd, k).wait_send(), x)[1], 0
                )
            ag_src[rnd] = value
            lax.fori_loop(
                0, R - 1 - me, lambda k, x: (ag_copy(rnd, R - 1 - k).start(), x)[1], 0
            )
            ag_buf[rnd, slot] = value

        def arrive(s, carry):
            pltpu.make_async_remote_copy(
                src_ref=ag_src.at[rnd], dst_ref=ag_buf.at[rnd, s],
                send_sem=ag_send.at[0], recv_sem=ag_recv.at[rnd, s],
                device_id=(me, col), device_id_type=MESH,
            ).wait_recv()
            return carry

        lax.fori_loop(0, before, arrive, 0)

    def multiply(rnd, masks):
        zero = jnp.zeros((b.shape[0], T), jnp.bfloat16)
        parts = [jnp.where(masks[s], ag_buf[rnd, s], zero) for s in range(CT)]
        return lax.dot_general(
            jnp.concatenate(parts, axis=1), a_ref[...], NT_DIMS,
            preferred_element_type=jnp.float32,
        )

    def comb_copy(rnd, step):
        to = lax.rem(col + step, C)
        return pltpu.make_async_remote_copy(
            src_ref=comb_buf.at[rnd, col], dst_ref=comb_buf.at[rnd, col],
            send_sem=comb_send.at[rnd, step], recv_sem=comb_recv.at[rnd, col],
            device_id=(me, to), device_id_type=MESH,
        )

    def combine(rnd, partial):
        comb_buf[rnd, col] = partial
        for step in range(1, C):
            comb_copy(rnd, step).start()
        for step in range(1, C):
            origin = lax.rem(col + step, C)
            pltpu.make_async_remote_copy(
                src_ref=comb_buf.at[rnd, col], dst_ref=comb_buf.at[rnd, origin],
                send_sem=comb_send.at[rnd, step], recv_sem=comb_recv.at[rnd, origin],
                device_id=(me, origin), device_id_type=MESH,
            ).wait_recv()
        out = comb_buf[rnd, 0]
        for c in range(1, C):
            out = out + comb_buf[rnd, c]
        return out

    zeros = jnp.zeros(b.shape, jnp.float32)
    forward = zeros
    correction = zeros
    rnd = 0
    for level in range(LEVELS - 1, -1, -1):
        here = row_level == level
        gather(rnd, (b - correction).astype(jnp.bfloat16))
        solved = combine(rnd, multiply(rnd, same))
        solved = jnp.where(here, solved, zeros)
        forward = forward + solved
        rnd += 1
        if level > 0:
            gather(rnd, solved.astype(jnp.bfloat16))
            correction = correction + combine(rnd, multiply(rnd, linked))
            rnd += 1
    fwd_ref[:, 0, :] = forward
    rounded = forward.astype(jnp.bfloat16)
    base = rounded.astype(jnp.float32)

    def rs_copy(rnd, s):
        return pltpu.make_async_remote_copy(
            src_ref=rs_src.at[rnd, s], dst_ref=rs_buf.at[rnd, me],
            send_sem=rs_send.at[rnd, s], recv_sem=rs_recv.at[rnd, me],
            device_id=(s * C + col, col), device_id_type=MESH,
        )

    def scatter(rnd, value, masks):
        blocks = lax.dot_general(
            value, a_ref[...], NN_DIMS, preferred_element_type=jnp.float32
        )
        for s in range(CT):
            rs_src[rnd, s] = jnp.where(
                masks[s], blocks[:, s * T:(s + 1) * T], zeros
            ).astype(jnp.bfloat16)
        lax.fori_loop(0, before, lambda s, x: (rs_copy(rnd, s).start(), x)[1], 0)

    def reduce(rnd):
        def arrive(k, carry):
            pltpu.make_async_remote_copy(
                src_ref=rs_src.at[rnd, 0], dst_ref=rs_buf.at[rnd, k],
                send_sem=rs_send.at[rnd, 0], recv_sem=rs_recv.at[rnd, k],
                device_id=(k, col), device_id_type=MESH,
            ).wait_recv()
            return carry

        lax.fori_loop(me + 1, R, arrive, 0)
        out = rs_src[rnd, slot].astype(jnp.float32)
        for k in range(R):
            out = out + rs_buf[rnd, k].astype(jnp.float32)
        return out

    def share_copy(rnd, step):
        return pltpu.make_async_remote_copy(
            src_ref=share_buf.at[rnd], dst_ref=share_buf.at[rnd],
            send_sem=share_send.at[rnd, step], recv_sem=share_recv.at[rnd],
            device_id=(me, lax.rem(col + step, C)), device_id_type=MESH,
        )

    def share(rnd, finish):
        @pl.when(mine)
        def _():
            share_buf[rnd] = finish(reduce(rnd))
            for step in range(1, C):
                share_copy(rnd, step).start()

        if C > 1:
            @pl.when(jnp.logical_not(mine))
            def _():
                share_copy(rnd, 1).wait_recv()

        return share_buf[rnd]

    fin_src[...] = zeros
    update = zeros
    rnd = 0
    current = jnp.where(row_level == 0, rounded, jnp.zeros_like(rounded))
    for level in range(LEVELS):
        scatter(rnd, current, same)
        if level < LEVELS - 1:
            def keep(value):
                fin_src[...] = fin_src[...] + value
                return value

            solved = share(rnd, keep).astype(jnp.bfloat16)
            rnd += 1
            scatter(rnd, solved, linked)
            update = update + share(rnd, lambda value: value)
            rnd += 1
            current = jnp.where(
                row_level == level + 1, base - update, zeros
            ).astype(jnp.bfloat16)

    def fin_copy(step):
        return pltpu.make_async_remote_copy(
            src_ref=fin_buf.at[slot], dst_ref=fin_buf.at[slot],
            send_sem=fin_send.at[step], recv_sem=fin_recv.at[slot],
            device_id=(lax.rem(me + step, R), col), device_id_type=MESH,
        )

    @pl.when(mine)
    def _():
        fin_buf[slot] = (fin_src[...] + reduce(rnd)).astype(jnp.bfloat16)
        lax.fori_loop(1, R, lambda step, x: (fin_copy(step).start(), x)[1], 0)

    def fin_arrive(s, carry):
        @pl.when(s * C + col != me)
        def _():
            pltpu.make_async_remote_copy(
                src_ref=fin_buf.at[s], dst_ref=fin_buf.at[s],
                send_sem=fin_send.at[0], recv_sem=fin_recv.at[s],
                device_id=(me, col), device_id_type=MESH,
            ).wait_recv()
        return carry

    for r in range(comb_buf.shape[0]):
        for step in range(1, C):
            comb_copy(r, step).wait_send()
    for r in range(rs_buf.shape[0]):
        lax.fori_loop(0, before, lambda s, x: (rs_copy(r, s).wait_send(), x)[1], 0)

    @pl.when(mine)
    def _():
        lax.fori_loop(me + 1, R, lambda k, x: (ag_copy(0, k).wait_send(), x)[1], 0)
        for r in range(share_buf.shape[0]):
            for step in range(1, C):
                share_copy(r, step).wait_send()

    lax.fori_loop(0, CT, fin_arrive, 0)
    for s in range(CT):
        sol_ref[:, s, :] = fin_buf[s].astype(jnp.float32)

    @pl.when(mine)
    def _():
        lax.fori_loop(1, R, lambda step, x: (fin_copy(step).wait_send(), x)[1], 0)


def shards(R, C, right_sides, factor, node_sizes, row_blocks):
    rhs, row_tiles, T = right_sides.shape
    rows, CT = factor.shape[1], factor.shape[2]
    levels = (node_sizes.shape[0] + 1).bit_length() - 1
    assert row_tiles == 1 and rows == T and CT * C == R
    rounds = 2 * levels - 1
    matrix = factor.reshape(rows, CT * T)
    vmem = pl.BlockSpec(memory_space=pltpu.VMEM)
    smem = pl.BlockSpec(memory_space=pltpu.SMEM)
    dma = pltpu.SemaphoreType.DMA
    bf16, f32 = jnp.bfloat16, jnp.float32
    return pl.pallas_call(
        functools.partial(kernel, R, C, CT, levels),
        out_shape=(
            jax.ShapeDtypeStruct((rhs, 1, T), f32),
            jax.ShapeDtypeStruct((rhs, CT, T), f32),
        ),
        in_specs=[smem, smem, vmem, vmem],
        out_specs=(vmem, vmem),
        scratch_shapes=[
            pltpu.VMEM((rounds, rhs, T), bf16),
            pltpu.VMEM((rounds, CT, rhs, T), bf16),
            pltpu.VMEM((rounds, C, rhs, T), f32),
            pltpu.VMEM((rounds, CT, rhs, T), bf16),
            pltpu.VMEM((rounds, R, rhs, T), bf16),
            pltpu.VMEM((rounds - 1, rhs, T), f32),
            pltpu.VMEM((rhs, T), f32),
            pltpu.VMEM((CT, rhs, T), bf16),
            dma((R,)),
            dma((rounds, CT)),
            dma((rounds, C)),
            dma((rounds, C)),
            dma((rounds, CT)),
            dma((rounds, R)),
            dma((rounds - 1, C)),
            dma((rounds - 1,)),
            dma((R,)),
            dma((CT,)),
        ],
        compiler_params=pltpu.CompilerParams(collective_id=0, has_side_effects=True),
        name="tree_solve",
    )(node_sizes, row_blocks, right_sides, matrix)


def solution(mesh):
    in_specs = (P(None, None, "prow"), P(None, "prow", None, "pcol"), P(), P())
    out_specs = (P(None, None, "prow"), P(None, None, "pcol"))
    body = functools.partial(shards, mesh.shape["prow"], mesh.shape["pcol"])
    return jax.shard_map(
        body, mesh=mesh, in_specs=in_specs, out_specs=out_specs, check_vma=False
    )
```

```python
import functools

import jax
import jax.numpy as jnp
from jax import lax
from jax.experimental import pallas as pl
from jax.experimental.pallas import tpu as pltpu
from jax.sharding import PartitionSpec as P

MESH = pl.DeviceIdType.MESH
NT_DIMS = (((1,), (1,)), ((), ()))
GROUP = 2
SPLIT = 2
CHUNK = 64
LANES = 128
NN_DIMS = (((1,), (0,)), ((), ()))


def kernel(
    R, C, CT, LEVELS,
    sizes_ref, blocks_ref, b_ref, factor_ref,
    fwd_ref, sol_ref,
    raw, wide, a_ref,
    ag_src, ag_buf, comb_buf, rs_src, rs_buf, share_buf, fin_src, fin_buf, update,
    ag_send, ag_recv, comb_send, comb_recv, rs_send, rs_recv,
    share_send, share_recv, fin_send, fin_recv, load_sem,
):
    SN = sizes_ref.shape[0]
    me = lax.axis_index("prow")
    col = lax.axis_index("pcol")
    mine = lax.rem(me, C) == col
    slot = me // C
    before = (me + C - 1 - col) // C
    T = b_ref.shape[2]

    load = pltpu.make_async_copy(factor_ref.at[0], raw, load_sem)
    load.start()
    barrier = pltpu.get_barrier_semaphore()

    def greet_row(step, carry):
        pl.semaphore_signal(
            barrier, inc=1, device_id=(lax.rem(me + step, R), col), device_id_type=MESH
        )
        return carry

    def greet_col(step, carry):
        pl.semaphore_signal(
            barrier, inc=1, device_id=(me, lax.rem(col + step, C)), device_id_type=MESH
        )
        return carry

    lax.fori_loop(1, R, greet_row, 0)
    lax.fori_loop(1, C, greet_col, 0)

    ends = []
    total = jnp.int32(0)
    for s in range(SN):
        total = total + sizes_ref[s]
        ends.append(total)

    def node_of(tile):
        count = jnp.int32(0)
        for s in range(SN):
            count = count + jnp.where(ends[s] <= tile, 1, 0)
        return jnp.minimum(count, SN - 1)

    row_node = node_of(me)
    row_label = SN - row_node
    row_level = jnp.int32(0)
    for e in range(1, LEVELS):
        row_level = row_level + jnp.where(row_label >= 2**e, 1, 0)
    same, linked = [], []
    for s in range(CT):
        node = node_of(s * C + col)
        label = SN - node
        above = jnp.int32(0)
        for gap in range(1, LEVELS):
            above = above + jnp.where(jnp.right_shift(label, gap) == row_label, 1, 0)
        flag = jnp.where(blocks_ref[node, me] == 1, 1, 0)
        low = jnp.where(s * C + col <= me, 1, 0)
        same.append(jnp.where(node == row_node, 1, 0) * low > 0)
        linked.append(above * flag * low > 0)

    b = b_ref[:, 0, :]
    pl.semaphore_wait(barrier, R - 1 + C - 1)

    def relayout(step, carry):
        start = pl.multiple_of(step * CHUNK, CHUNK)
        rows = pl.ds(start, CHUNK)
        for h in range(T // LANES):
            block = raw[rows, :, h * LANES:(h + 1) * LANES].astype(jnp.float32)
            wide[h] = block.reshape(CHUNK * CT, LANES)
        for s in range(CT):
            for h in range(T // LANES):
                part = wide[h, pl.ds(s, CHUNK, stride=CT), :]
                at = s * T + h * LANES
                a_ref[rows, at:at + LANES] = part.astype(jnp.bfloat16)
        return carry

    def ag_copy(rnd, k):
        return pltpu.make_async_remote_copy(
            src_ref=ag_src.at[rnd], dst_ref=ag_buf.at[rnd, slot],
            send_sem=ag_send.at[k], recv_sem=ag_recv.at[rnd, slot],
            device_id=(k, col), device_id_type=MESH,
        )

    def send_row(rnd, value):
        @pl.when(mine)
        def _():
            if rnd > 0:
                lax.fori_loop(
                    me + 1, R, lambda k, x: (ag_copy(rnd, k).wait_send(), x)[1], 0
                )
            ag_src[rnd] = value
            lax.fori_loop(
                me + 1, R, lambda k, x: (ag_copy(rnd, k).start(), x)[1], 0
            )
            ag_buf[rnd, slot] = value

    def arrive_at(rnd, s):
        pltpu.make_async_remote_copy(
            src_ref=ag_src.at[rnd], dst_ref=ag_buf.at[rnd, s],
            send_sem=ag_send.at[0], recv_sem=ag_recv.at[rnd, s],
            device_id=(me, col), device_id_type=MESH,
        ).wait_recv()

    def multiply(rnd, masks):
        zero = jnp.zeros((b.shape[0], T), jnp.bfloat16)
        out = None
        for last in range(CT, 0, -GROUP):
            group = range(max(last - GROUP, 0), last)
            for s in reversed(group):
                pl.when(s < before)(functools.partial(arrive_at, rnd, s))
            parts = [jnp.where(masks[s], ag_buf[rnd, s], zero) for s in group]
            value = lax.dot_general(
                jnp.concatenate(parts, axis=1), a_ref[:, group[0] * T:last * T], NT_DIMS,
                preferred_element_type=jnp.float32,
            )
            out = value if out is None else out + value
        return out

    def comb_copy(rnd, step):
        to = lax.rem(col + step, C)
        return pltpu.make_async_remote_copy(
            src_ref=comb_buf.at[rnd, col], dst_ref=comb_buf.at[rnd, col],
            send_sem=comb_send.at[rnd, step], recv_sem=comb_recv.at[rnd, col],
            device_id=(me, to), device_id_type=MESH,
        )

    def combine(rnd, partial):
        comb_buf[rnd, col] = partial
        for step in range(1, C):
            comb_copy(rnd, step).start()
        for step in range(1, C):
            origin = lax.rem(col + step, C)
            pltpu.make_async_remote_copy(
                src_ref=comb_buf.at[rnd, col], dst_ref=comb_buf.at[rnd, origin],
                send_sem=comb_send.at[rnd, step], recv_sem=comb_recv.at[rnd, origin],
                device_id=(me, origin), device_id_type=MESH,
            ).wait_recv()
        out = comb_buf[rnd, 0]
        for c in range(1, C):
            out = out + comb_buf[rnd, c]
        return out

    zeros = jnp.zeros(b.shape, jnp.float32)
    forward = zeros
    correction = zeros
    rnd = 0
    for level in range(LEVELS - 1, -1, -1):
        here = row_level == level
        send_row(rnd, (b - correction).astype(jnp.bfloat16))
        if rnd == 0:
            load.wait()
            lax.fori_loop(0, T // CHUNK, relayout, 0)
        solved = combine(rnd, multiply(rnd, same))
        solved = jnp.where(here, solved, zeros)
        forward = forward + solved
        rnd += 1
        if level > 0:
            send_row(rnd, solved.astype(jnp.bfloat16))
            correction = correction + combine(rnd, multiply(rnd, linked))
            rnd += 1
    fwd_ref[...] = forward
    rounded = forward.astype(jnp.bfloat16)
    base = rounded.astype(jnp.float32)

    def rs_copy(rnd, s):
        return pltpu.make_async_remote_copy(
            src_ref=rs_src.at[rnd, s], dst_ref=rs_buf.at[rnd, me],
            send_sem=rs_send.at[rnd, s], recv_sem=rs_recv.at[rnd, me],
            device_id=(s * C + col, col), device_id_type=MESH,
        )

    def scatter(rnd, value, masks):
        for last in range(CT, 0, -SPLIT):
            first = max(last - SPLIT, 0)
            blocks = lax.dot_general(
                value, a_ref[:, first * T:last * T], NN_DIMS,
                preferred_element_type=jnp.float32,
            )
            for s in reversed(range(first, last)):
                rs_src[rnd, s] = jnp.where(
                    masks[s], blocks[:, (s - first) * T:(s - first + 1) * T], zeros
                ).astype(jnp.bfloat16)
                pl.when(s < before)(rs_copy(rnd, s).start)

    def reduce(rnd):
        def arrive(k, carry):
            pltpu.make_async_remote_copy(
                src_ref=rs_src.at[rnd, 0], dst_ref=rs_buf.at[rnd, k],
                send_sem=rs_send.at[rnd, 0], recv_sem=rs_recv.at[rnd, k],
                device_id=(k, col), device_id_type=MESH,
            ).wait_recv()
            return carry + rs_buf[rnd, k].astype(jnp.float32)

        return lax.fori_loop(me + 1, R, arrive, rs_src[rnd, slot].astype(jnp.float32))

    def share_copy(rnd, step):
        return pltpu.make_async_remote_copy(
            src_ref=share_buf.at[rnd], dst_ref=share_buf.at[rnd],
            send_sem=share_send.at[rnd, step], recv_sem=share_recv.at[rnd],
            device_id=(me, lax.rem(col + step, C)), device_id_type=MESH,
        )

    def share(rnd, finish):
        @pl.when(mine)
        def _():
            share_buf[rnd] = finish(reduce(rnd)).astype(jnp.bfloat16)
            for step in range(1, C):
                share_copy(rnd, step).start()

        if C > 1:
            @pl.when(jnp.logical_not(mine))
            def _():
                share_copy(rnd, 1).wait_recv()

        return share_buf[rnd]

    fin_src[...] = zeros
    update[...] = zeros
    rnd = 0
    current = jnp.where(row_level == 0, rounded, jnp.zeros_like(rounded))
    for level in range(LEVELS - 1):
        scatter(rnd, current, same)

        def keep(value):
            fin_src[...] = fin_src[...] + value
            return value

        solved = share(rnd, keep)
        rnd += 1
        scatter(rnd, solved, linked)

        def settle(value):
            update[...] = update[...] + value
            return jnp.where(row_level == level + 1, base - update[...], zeros)

        current = share(rnd, settle)
        rnd += 1
    scatter(rnd, current, same)

    def fin_copy(step):
        return pltpu.make_async_remote_copy(
            src_ref=fin_buf.at[slot], dst_ref=fin_buf.at[slot],
            send_sem=fin_send.at[step], recv_sem=fin_recv.at[slot],
            device_id=(lax.rem(me + step, R), col), device_id_type=MESH,
        )

    @pl.when(mine)
    def _():
        fin_buf[slot] = (fin_src[...] + reduce(rnd)).astype(jnp.bfloat16)
        lax.fori_loop(1, R, lambda step, x: (fin_copy(step).start(), x)[1], 0)

    def fin_arrive(s, carry):
        @pl.when(s * C + col != me)
        def _():
            pltpu.make_async_remote_copy(
                src_ref=fin_buf.at[s], dst_ref=fin_buf.at[s],
                send_sem=fin_send.at[0], recv_sem=fin_recv.at[s],
                device_id=(me, col), device_id_type=MESH,
            ).wait_recv()
        return carry

    for r in range(comb_buf.shape[0]):
        for step in range(1, C):
            comb_copy(r, step).wait_send()
    for r in range(rs_buf.shape[0]):
        lax.fori_loop(0, before, lambda s, x: (rs_copy(r, s).wait_send(), x)[1], 0)

    @pl.when(mine)
    def _():
        lax.fori_loop(me + 1, R, lambda k, x: (ag_copy(0, k).wait_send(), x)[1], 0)
        for r in range(share_buf.shape[0]):
            for step in range(1, C):
                share_copy(r, step).wait_send()

    lax.fori_loop(0, CT, fin_arrive, 0)
    for s in range(CT):
        sol_ref[s] = fin_buf[s]

    @pl.when(mine)
    def _():
        lax.fori_loop(1, R, lambda step, x: (fin_copy(step).wait_send(), x)[1], 0)


def finish_kernel(rows_ref, tiles_ref, fwd_ref, sol_ref):
    fwd_ref[:, 0, :] = rows_ref[...]
    for s in range(tiles_ref.shape[0]):
        sol_ref[:, s, :] = tiles_ref[s].astype(jnp.float32)


def shards(R, C, right_sides, factor, node_sizes, row_blocks):
    rhs, row_tiles, T = right_sides.shape
    rows, CT = factor.shape[1], factor.shape[2]
    levels = (node_sizes.shape[0] + 1).bit_length() - 1
    assert row_tiles == 1 and rows == T and CT * C == R
    rounds = 2 * levels - 1
    vmem = pl.BlockSpec(memory_space=pltpu.VMEM)
    smem = pl.BlockSpec(memory_space=pltpu.SMEM)
    dma = pltpu.SemaphoreType.DMA
    bf16, f32 = jnp.bfloat16, jnp.float32
    forward, tiles = pl.pallas_call(
        functools.partial(kernel, R, C, CT, levels),
        out_shape=(
            jax.ShapeDtypeStruct((rhs, T), f32),
            jax.ShapeDtypeStruct((CT, rhs, T), bf16),
        ),
        in_specs=[smem, smem, vmem, pl.BlockSpec(memory_space=pl.ANY)],
        out_specs=(vmem, vmem),
        scratch_shapes=[
            pltpu.VMEM((rows, CT, T), bf16),
            pltpu.VMEM((T // LANES, CHUNK * CT, LANES), f32),
            pltpu.VMEM((rows, CT * T), bf16),
            pltpu.VMEM((rounds, rhs, T), bf16),
            pltpu.VMEM((rounds, CT, rhs, T), bf16),
            pltpu.VMEM((rounds, C, rhs, T), f32),
            pltpu.VMEM((rounds, CT, rhs, T), bf16),
            pltpu.VMEM((rounds, R, rhs, T), bf16),
            pltpu.VMEM((rounds - 1, rhs, T), bf16),
            pltpu.VMEM((rhs, T), f32),
            pltpu.VMEM((CT, rhs, T), bf16),
            pltpu.VMEM((rhs, T), f32),
            dma((R,)),
            dma((rounds, CT)),
            dma((rounds, C)),
            dma((rounds, C)),
            dma((rounds, CT)),
            dma((rounds, R)),
            dma((rounds - 1, C)),
            dma((rounds - 1,)),
            dma((R,)),
            dma((CT,)),
            dma,
        ],
        compiler_params=pltpu.CompilerParams(collective_id=0, has_side_effects=True),
        name="tree_solve",
    )(node_sizes, row_blocks, right_sides, factor)

    return pl.pallas_call(
        finish_kernel,
        out_shape=(
            jax.ShapeDtypeStruct((rhs, 1, T), f32),
            jax.ShapeDtypeStruct((rhs, CT, T), f32),
        ),
        in_specs=[vmem, vmem],
        out_specs=(vmem, vmem),
        name="place",
    )(forward, tiles)


def solution(mesh):
    in_specs = (P(None, None, "prow"), P(None, "prow", None, "pcol"), P(), P())
    out_specs = (P(None, None, "prow"), P(None, None, "pcol"))
    body = functools.partial(shards, mesh.shape["prow"], mesh.shape["pcol"])
    return jax.shard_map(
        body, mesh=mesh, in_specs=in_specs, out_specs=out_specs, check_vma=False
    )
```

```python
import functools

import jax
import jax.numpy as jnp
from jax import lax
from jax.experimental import pallas as pl
from jax.experimental.pallas import tpu as pltpu
from jax.sharding import PartitionSpec as P

MESH = pl.DeviceIdType.MESH
NT_DIMS = (((1,), (1,)), ((), ()))
GROUP = 2
SPLIT = 8
CHUNK = 64
LANES = 128
NN_DIMS = (((1,), (0,)), ((), ()))


def kernel(
    R, C, CT, LEVELS,
    sizes_ref, blocks_ref, b_ref, factor_ref,
    fwd_ref, sol_ref,
    raw, wide, a_ref,
    ag_src, ag_buf, comb_buf, rs_src, rs_buf, share_buf, fin_src, fin_buf, update,
    ag_send, ag_recv, comb_send, comb_recv, rs_send, rs_recv,
    share_send, share_recv, fin_send, fin_recv, load_sem,
):
    SN = sizes_ref.shape[0]
    me = lax.axis_index("prow")
    col = lax.axis_index("pcol")
    mine = lax.rem(me, C) == col
    slot = me // C
    before = (me + C - 1 - col) // C
    T = b_ref.shape[2]

    load = pltpu.make_async_copy(factor_ref.at[0], raw, load_sem)
    load.start()
    barrier = pltpu.get_barrier_semaphore()

    def greet_row(step, carry):
        pl.semaphore_signal(
            barrier, inc=1, device_id=(lax.rem(me + step, R), col), device_id_type=MESH
        )
        return carry

    def greet_col(step, carry):
        pl.semaphore_signal(
            barrier, inc=1, device_id=(me, lax.rem(col + step, C)), device_id_type=MESH
        )
        return carry

    lax.fori_loop(1, R, greet_row, 0)
    lax.fori_loop(1, C, greet_col, 0)

    ends = []
    total = jnp.int32(0)
    for s in range(SN):
        total = total + sizes_ref[s]
        ends.append(total)

    def node_of(tile):
        count = jnp.int32(0)
        for s in range(SN):
            count = count + jnp.where(ends[s] <= tile, 1, 0)
        return jnp.minimum(count, SN - 1)

    row_node = node_of(me)
    row_label = SN - row_node
    row_level = jnp.int32(0)
    for e in range(1, LEVELS):
        row_level = row_level + jnp.where(row_label >= 2**e, 1, 0)
    same, linked = [], []
    for s in range(CT):
        node = node_of(s * C + col)
        label = SN - node
        above = jnp.int32(0)
        for gap in range(1, LEVELS):
            above = above + jnp.where(jnp.right_shift(label, gap) == row_label, 1, 0)
        flag = jnp.where(blocks_ref[node, me] == 1, 1, 0)
        low = jnp.where(s * C + col <= me, 1, 0)
        same.append(jnp.where(node == row_node, 1, 0) * low > 0)
        linked.append(above * flag * low > 0)

    b = b_ref[:, 0, :]
    pl.semaphore_wait(barrier, R - 1 + C - 1)

    def relayout(step, carry):
        start = pl.multiple_of(step * CHUNK, CHUNK)
        rows = pl.ds(start, CHUNK)
        for h in range(T // LANES):
            block = raw[rows, :, h * LANES:(h + 1) * LANES].astype(jnp.float32)
            wide[h] = block.reshape(CHUNK * CT, LANES)
        for s in range(CT):
            for h in range(T // LANES):
                part = wide[h, pl.ds(s, CHUNK, stride=CT), :]
                at = s * T + h * LANES
                a_ref[rows, at:at + LANES] = part.astype(jnp.bfloat16)
        return carry

    def ag_copy(rnd, k):
        return pltpu.make_async_remote_copy(
            src_ref=ag_src.at[rnd], dst_ref=ag_buf.at[rnd, slot],
            send_sem=ag_send.at[k], recv_sem=ag_recv.at[rnd, slot],
            device_id=(k, col), device_id_type=MESH,
        )

    def send_row(rnd, value):
        @pl.when(mine)
        def _():
            if rnd > 0:
                lax.fori_loop(
                    me + 1, R, lambda k, x: (ag_copy(rnd, k).wait_send(), x)[1], 0
                )
            ag_src[rnd] = value
            lax.fori_loop(
                me + 1, R, lambda k, x: (ag_copy(rnd, k).start(), x)[1], 0
            )
            ag_buf[rnd, slot] = value

    def arrive_at(rnd, s):
        pltpu.make_async_remote_copy(
            src_ref=ag_src.at[rnd], dst_ref=ag_buf.at[rnd, s],
            send_sem=ag_send.at[0], recv_sem=ag_recv.at[rnd, s],
            device_id=(me, col), device_id_type=MESH,
        ).wait_recv()

    def multiply(rnd, masks):
        zero = jnp.zeros((b.shape[0], T), jnp.bfloat16)
        out = None
        for last in range(CT, 0, -GROUP):
            group = range(max(last - GROUP, 0), last)
            for s in reversed(group):
                pl.when(s < before)(functools.partial(arrive_at, rnd, s))
            parts = [jnp.where(masks[s], ag_buf[rnd, s], zero) for s in group]
            value = lax.dot_general(
                jnp.concatenate(parts, axis=1), a_ref[:, group[0] * T:last * T], NT_DIMS,
                preferred_element_type=jnp.float32,
            )
            out = value if out is None else out + value
        return out

    def comb_copy(rnd, step):
        to = lax.rem(col + step, C)
        return pltpu.make_async_remote_copy(
            src_ref=comb_buf.at[rnd, col], dst_ref=comb_buf.at[rnd, col],
            send_sem=comb_send.at[rnd, step], recv_sem=comb_recv.at[rnd, col],
            device_id=(me, to), device_id_type=MESH,
        )

    def combine(rnd, partial):
        comb_buf[rnd, col] = partial
        for step in range(1, C):
            comb_copy(rnd, step).start()
        for step in range(1, C):
            origin = lax.rem(col + step, C)
            pltpu.make_async_remote_copy(
                src_ref=comb_buf.at[rnd, col], dst_ref=comb_buf.at[rnd, origin],
                send_sem=comb_send.at[rnd, step], recv_sem=comb_recv.at[rnd, origin],
                device_id=(me, origin), device_id_type=MESH,
            ).wait_recv()
        out = comb_buf[rnd, 0]
        for c in range(1, C):
            out = out + comb_buf[rnd, c]
        return out

    zeros = jnp.zeros(b.shape, jnp.float32)
    forward = zeros
    correction = zeros
    rnd = 0
    for level in range(LEVELS - 1, -1, -1):
        here = row_level == level
        send_row(rnd, (b - correction).astype(jnp.bfloat16))
        if rnd == 0:
            load.wait()
            lax.fori_loop(0, T // CHUNK, relayout, 0)
        solved = combine(rnd, multiply(rnd, same))
        solved = jnp.where(here, solved, zeros)
        forward = forward + solved
        rnd += 1
        if level > 0:
            send_row(rnd, solved.astype(jnp.bfloat16))
            correction = correction + combine(rnd, multiply(rnd, linked))
            rnd += 1
    fwd_ref[...] = forward
    rounded = forward.astype(jnp.bfloat16)
    base = rounded.astype(jnp.float32)

    def rs_copy(rnd, s):
        return pltpu.make_async_remote_copy(
            src_ref=rs_src.at[rnd, s], dst_ref=rs_buf.at[rnd, me],
            send_sem=rs_send.at[rnd, s], recv_sem=rs_recv.at[rnd, me],
            device_id=(s * C + col, col), device_id_type=MESH,
        )

    def scatter(rnd, value, masks):
        for last in range(CT, 0, -SPLIT):
            first = max(last - SPLIT, 0)
            blocks = lax.dot_general(
                value, a_ref[:, first * T:last * T], NN_DIMS,
                preferred_element_type=jnp.float32,
            )
            for s in reversed(range(first, last)):
                rs_src[rnd, s] = jnp.where(
                    masks[s], blocks[:, (s - first) * T:(s - first + 1) * T], zeros
                ).astype(jnp.bfloat16)
                pl.when(s < before)(rs_copy(rnd, s).start)

    def reduce(rnd):
        def arrive(k, carry):
            pltpu.make_async_remote_copy(
                src_ref=rs_src.at[rnd, 0], dst_ref=rs_buf.at[rnd, k],
                send_sem=rs_send.at[rnd, 0], recv_sem=rs_recv.at[rnd, k],
                device_id=(k, col), device_id_type=MESH,
            ).wait_recv()
            return carry + rs_buf[rnd, k].astype(jnp.float32)

        return lax.fori_loop(me + 1, R, arrive, rs_src[rnd, slot].astype(jnp.float32))

    def share_copy(rnd, step):
        return pltpu.make_async_remote_copy(
            src_ref=share_buf.at[rnd], dst_ref=share_buf.at[rnd],
            send_sem=share_send.at[rnd, step], recv_sem=share_recv.at[rnd],
            device_id=(me, lax.rem(col + step, C)), device_id_type=MESH,
        )

    def share(rnd, finish):
        @pl.when(mine)
        def _():
            share_buf[rnd] = finish(reduce(rnd)).astype(jnp.bfloat16)
            for step in range(1, C):
                share_copy(rnd, step).start()

        if C > 1:
            @pl.when(jnp.logical_not(mine))
            def _():
                share_copy(rnd, 1).wait_recv()

        return share_buf[rnd]

    fin_src[...] = zeros
    update[...] = zeros
    rnd = 0
    current = jnp.where(row_level == 0, rounded, jnp.zeros_like(rounded))
    for level in range(LEVELS - 1):
        scatter(rnd, current, same)

        def keep(value):
            fin_src[...] = fin_src[...] + value
            return value

        solved = share(rnd, keep)
        rnd += 1
        scatter(rnd, solved, linked)

        def settle(value):
            update[...] = update[...] + value
            return jnp.where(row_level == level + 1, base - update[...], zeros)

        current = share(rnd, settle)
        rnd += 1
    scatter(rnd, current, same)

    def fin_copy(step):
        return pltpu.make_async_remote_copy(
            src_ref=fin_buf.at[slot], dst_ref=fin_buf.at[slot],
            send_sem=fin_send.at[step], recv_sem=fin_recv.at[slot],
            device_id=(lax.rem(me + step, R), col), device_id_type=MESH,
        )

    @pl.when(mine)
    def _():
        fin_buf[slot] = (fin_src[...] + reduce(rnd)).astype(jnp.bfloat16)
        lax.fori_loop(1, R, lambda step, x: (fin_copy(step).start(), x)[1], 0)

    def fin_arrive(s, carry):
        @pl.when(s * C + col != me)
        def _():
            pltpu.make_async_remote_copy(
                src_ref=fin_buf.at[s], dst_ref=fin_buf.at[s],
                send_sem=fin_send.at[0], recv_sem=fin_recv.at[s],
                device_id=(me, col), device_id_type=MESH,
            ).wait_recv()
        return carry

    for r in range(comb_buf.shape[0]):
        for step in range(1, C):
            comb_copy(r, step).wait_send()
    for r in range(rs_buf.shape[0]):
        lax.fori_loop(0, before, lambda s, x: (rs_copy(r, s).wait_send(), x)[1], 0)

    @pl.when(mine)
    def _():
        lax.fori_loop(me + 1, R, lambda k, x: (ag_copy(0, k).wait_send(), x)[1], 0)
        for r in range(share_buf.shape[0]):
            for step in range(1, C):
                share_copy(r, step).wait_send()

    lax.fori_loop(0, CT, fin_arrive, 0)
    for s in range(CT):
        sol_ref[s] = fin_buf[s]

    @pl.when(mine)
    def _():
        lax.fori_loop(1, R, lambda step, x: (fin_copy(step).wait_send(), x)[1], 0)


def finish_kernel(rows_ref, tiles_ref, fwd_ref, sol_ref):
    fwd_ref[:, 0, :] = rows_ref[...]
    for s in range(tiles_ref.shape[0]):
        sol_ref[:, s, :] = tiles_ref[s].astype(jnp.float32)


def shards(R, C, right_sides, factor, node_sizes, row_blocks):
    rhs, row_tiles, T = right_sides.shape
    rows, CT = factor.shape[1], factor.shape[2]
    levels = (node_sizes.shape[0] + 1).bit_length() - 1
    assert row_tiles == 1 and rows == T and CT * C == R
    rounds = 2 * levels - 1
    vmem = pl.BlockSpec(memory_space=pltpu.VMEM)
    smem = pl.BlockSpec(memory_space=pltpu.SMEM)
    dma = pltpu.SemaphoreType.DMA
    bf16, f32 = jnp.bfloat16, jnp.float32
    forward, tiles = pl.pallas_call(
        functools.partial(kernel, R, C, CT, levels),
        out_shape=(
            jax.ShapeDtypeStruct((rhs, T), f32),
            jax.ShapeDtypeStruct((CT, rhs, T), bf16),
        ),
        in_specs=[smem, smem, vmem, pl.BlockSpec(memory_space=pl.ANY)],
        out_specs=(vmem, vmem),
        scratch_shapes=[
            pltpu.VMEM((rows, CT, T), bf16),
            pltpu.VMEM((T // LANES, CHUNK * CT, LANES), f32),
            pltpu.VMEM((rows, CT * T), bf16),
            pltpu.VMEM((rounds, rhs, T), bf16),
            pltpu.VMEM((rounds, CT, rhs, T), bf16),
            pltpu.VMEM((rounds, C, rhs, T), f32),
            pltpu.VMEM((rounds, CT, rhs, T), bf16),
            pltpu.VMEM((rounds, R, rhs, T), bf16),
            pltpu.VMEM((rounds - 1, rhs, T), bf16),
            pltpu.VMEM((rhs, T), f32),
            pltpu.VMEM((CT, rhs, T), bf16),
            pltpu.VMEM((rhs, T), f32),
            dma((R,)),
            dma((rounds, CT)),
            dma((rounds, C)),
            dma((rounds, C)),
            dma((rounds, CT)),
            dma((rounds, R)),
            dma((rounds - 1, C)),
            dma((rounds - 1,)),
            dma((R,)),
            dma((CT,)),
            dma,
        ],
        compiler_params=pltpu.CompilerParams(collective_id=0, has_side_effects=True),
        name="tree_solve",
    )(node_sizes, row_blocks, right_sides, factor)

    return pl.pallas_call(
        finish_kernel,
        out_shape=(
            jax.ShapeDtypeStruct((rhs, 1, T), f32),
            jax.ShapeDtypeStruct((rhs, CT, T), f32),
        ),
        in_specs=[vmem, vmem],
        out_specs=(vmem, vmem),
        name="place",
    )(forward, tiles)


def solution(mesh):
    in_specs = (P(None, None, "prow"), P(None, "prow", None, "pcol"), P(), P())
    out_specs = (P(None, None, "prow"), P(None, None, "pcol"))
    body = functools.partial(shards, mesh.shape["prow"], mesh.shape["pcol"])
    return jax.shard_map(
        body, mesh=mesh, in_specs=in_specs, out_specs=out_specs, check_vma=False
    )
```
